512 devices in a mesh: seq: 64 (over y_lo, z, x), fsdp: 8 (over y_hi, core).
Axes of the slice: x: 4, y: 8 (y_hi: 4, y_lo: 2; y = y_hi * 2 + y_lo), z: 8, core: 2. Of those that a mesh axis runs over, the one named last changes fastest.
Arguments:
- features: bfloat16 [8, 8192, 6144], P('fsdp', 'seq'), may hold values from -6 to 6
- short_taps: float32 [7, 384], replicated, may hold values from -2 to 2
- long_taps: float32 [128, 128], replicated, may hold values from -0.5 to 0.5
- out_weight: bfloat16 [2048, 4096], P(None, 'fsdp'), may hold values from -0.125 to 0.125
Outputs:
- mixer_out: bfloat16 [8, 8192, 4096], P('fsdp', 'seq')
The draws below stay inside these ranges and needn't reach their ends.
All inputs are finite; a program needn't handle non-finite values.
Results may differ from the reference program's by a relative error of at most 0.0057.
Values may be sent and summed in bfloat16 or wider, within the bound.
A program may use at most 128 MiB of HBM per device.

```python
import jax
import jax.numpy as jnp
from jax import lax

D = 4096
C = 2048
GROUP = 16
SHORT = 7
TAPS = 128
SEQS = 8
LENGTH = 8192


def block_levels(key, dims, shards, least, largest):
    loudness = 1.0
    for position, parts in shards:
        draws = jax.random.uniform(jax.random.fold_in(jax.random.fold_in(key, 6), position), (parts,), jnp.float32, least / len(shards), largest / len(shards))
        loudness = loudness * jnp.repeat(jnp.exp(draws), dims[position] // parts).reshape((-1,) + (1,) * (len(dims) - 1 - position))
    return loudness


def noise(own_key, extent, spread, limit, cuts=(), dtype=jnp.bfloat16):
    result = spread * jax.random.normal(own_key, extent, jnp.float32)
    if cuts:
        result = result * block_levels(own_key, extent, cuts, -0.22, 0.18)
    return jnp.clip(result, -limit, limit).astype(dtype)


def setup_inputs(seed: int = 0) -> dict:
    key_list = jax.random.split(jax.random.key(seed), 5)
    return {
        "features": noise(key_list[0], (SEQS, LENGTH, 3 * C), 1.0, 6.0, ((0, 8), (1, 64))),
        "short_taps": noise(key_list[1], (SHORT, 3 * C // GROUP), SHORT ** -0.5, 2.0, (), jnp.float32),
        "long_taps": noise(key_list[2], (TAPS, C // GROUP), TAPS ** -0.5, 0.5, (), jnp.float32),
        "out_weight": noise(key_list[3], (C, D), C ** -0.5, 0.125, ((1, 8),)),
    }


def reference(features, short_taps, long_taps, out_weight):
    short_table = jnp.repeat(short_taps, GROUP, axis=1)
    long_table = jnp.repeat(long_taps, GROUP, axis=1)

    def score_sequence(sequence_feats):
        padded = jnp.pad(sequence_feats, ((SHORT - 1, 0), (0, 0)))
        filtered = jnp.zeros((LENGTH, 3 * C), jnp.float32)
        for index_tap in range(SHORT):
            window_rows = padded[SHORT - 1 - index_tap:SHORT - 1 - index_tap + LENGTH].astype(jnp.float32)
            filtered = filtered + short_table[index_tap] * window_rows
        query_part = filtered[:, 0:C]
        product = (filtered[:, C:2 * C] * filtered[:, 2 * C:3 * C]).astype(jnp.bfloat16)
        product = lax.optimization_barrier(product)
        product_pad = jnp.pad(product.astype(jnp.float32), ((TAPS - 1, 0), (0, 0)))

        def add_tap(lag_index, total):
            shifted = lax.dynamic_slice_in_dim(product_pad, TAPS - 1 - lag_index, LENGTH, 0)
            return total + long_table[lag_index] * shifted

        mixed_long = lax.fori_loop(0, TAPS, add_tap, jnp.zeros((LENGTH, C), jnp.float32))
        gated = (query_part * mixed_long).astype(jnp.bfloat16)
        return jnp.dot(gated, out_weight, preferred_element_type=jnp.float32).astype(jnp.bfloat16)

    return lax.map(score_sequence, features)
```

```python
import functools

import jax
import jax.numpy as jnp
from jax import lax
from jax.experimental import pallas as pl
from jax.experimental.pallas import tpu as pltpu
from jax.sharding import PartitionSpec as P

MESH = pl.DeviceIdType.MESH
GROUP = 16
XN = 4
ZN = 8
LANES = 128
PIECES = 4
CHUNKS = 4
BF16 = jnp.bfloat16
F32 = jnp.float32


def kernel(
    seq_count,
    x_hbm,
    st_ref,
    lt_ref,
    w_hbm,
    out_ref,
    feat,
    fhalo,
    taps_s,
    taps_r,
    toep,
    qf,
    pown,
    phalo,
    wbuf,
    gat,
    res,
    loc_sem,
    fh_sem,
    ph_sem,
    y_sem,
    x_sem,
    g_sem,
    o_sem,
):
    rows = feat.shape[0]
    channels = qf.shape[1]
    depth = w_hbm.shape[0]
    shard = w_hbm.shape[1]
    piece = depth // PIECES
    chunk = channels // CHUNKS
    blocks = chunk // LANES
    per_block = LANES // GROUP
    half = shard // 2

    seq = lax.axis_index("seq")
    fs = lax.axis_index("fsdp")
    x = seq % XN
    z = (seq // XN) % ZN
    y_lo = seq // (XN * ZN)
    y_hi = fs // 2
    core = fs % 2
    u = x % 2
    p = z % 2
    delta = 2 * y_lo - 1
    seq_flip = seq - delta * (XN * ZN)
    hi_outer = (y_hi + delta + 4) % 4
    outer = (seq_flip, hi_outer * 2 + core)
    sibling = (seq_flip, fs)
    right = (seq - x + (x + 1) % XN, fs)
    left = (seq - x + (x + XN - 1) % XN, fs)
    seq_z = seq + XN * (1 - 2 * p)
    other = fs + 1 - 2 * core
    pool = (None, (seq, other), (seq_z, fs), (seq_z, other))
    following = (seq + 1, fs)
    previous = (seq - 1, fs)
    has_next = seq < seq_count - 1
    has_prev = seq > 0

    def remote(src, dst, send, recv, target):
        return pltpu.make_async_remote_copy(
            src_ref=src,
            dst_ref=dst,
            send_sem=send,
            recv_sem=recv,
            device_id=target,
            device_id_type=MESH,
        )

    feat_copy = pltpu.make_async_copy(x_hbm.at[0], feat, loc_sem.at[0])
    feat_copy.start()
    own_w = []
    for part in range(2):
        column = pl.multiple_of(half * p + LANES * part, LANES)
        copy = pltpu.make_async_copy(
            w_hbm.at[:, pl.ds(column, LANES)], wbuf.at[0, part], loc_sem.at[1 + part]
        )
        copy.start()
        own_w.append(copy)

    barrier = pltpu.get_barrier_semaphore()
    greeted = (outer, sibling, right, left) + pool[1:]
    greeted += (((seq + 1) % seq_count, fs), ((seq + seq_count - 1) % seq_count, fs))
    for target in greeted:
        pl.semaphore_signal(barrier, inc=1, device_id=target, device_id_type=MESH)
    pl.semaphore_wait(barrier, len(greeted))

    halo_rows = fhalo.shape[0]
    feature_halo = remote(
        x_hbm.at[0, pl.ds(rows - halo_rows, halo_rows)],
        fhalo,
        fh_sem.at[0],
        fh_sem.at[1],
        following,
    )

    @pl.when(has_next)
    def _():
        feature_halo.start()

    def y_copy(slot, k):
        at_rows = pl.ds(piece * k, piece)
        if slot == 1:
            column = pl.multiple_of(half * p + LANES * u, LANES)
            src = w_hbm.at[at_rows, pl.ds(column, LANES)]
        else:
            src = wbuf.at[slot - 1, u, at_rows]
        return remote(
            src,
            wbuf.at[slot, u, at_rows],
            y_sem.at[0, slot - 1, k],
            y_sem.at[1, slot - 1, k],
            sibling if slot == 2 else outer,
        )

    def x_copy(slot, k):
        at_rows = pl.ds(piece * k, piece)
        block = wbuf.at[slot, u, at_rows]
        return remote(
            block,
            block,
            x_sem.at[0, slot - 1, k],
            x_sem.at[1, slot - 1, k],
            right if k < PIECES // 2 else left,
        )

    def relay(slot, k):
        y_copy(slot, k).wait_recv()
        if slot < 3:
            y_copy(slot + 1, k).start()
        x_copy(slot, k).start()

    for k in range(PIECES):
        y_copy(1, k).start()

    lane = lax.broadcasted_iota(jnp.int32, (LANES, LANES), 1)
    row = lax.broadcasted_iota(jnp.int32, (LANES, LANES), 0)
    taps_r[...] = jnp.take_along_axis(lt_ref[...].T, (LANES - lane) % LANES, axis=1)

    def build(g, carry):
        spread = jnp.broadcast_to(taps_r[pl.ds(g, 1), :], (LANES, LANES))
        circ = pltpu.roll(spread, 0, 1, stride=1, stride_axis=0)
        high = circ.astype(BF16).astype(F32)
        low = circ - high
        below = lane <= row
        zero = jnp.zeros_like(circ)
        toep[g, :, 0:128] = jnp.where(below, zero, high).astype(BF16)
        toep[g, :, 128:256] = jnp.where(below, high, zero).astype(BF16)
        toep[g, :, 256:384] = jnp.where(below, zero, low).astype(BF16)
        toep[g, :, 384:512] = jnp.where(below, low, zero).astype(BF16)
        return carry

    lax.fori_loop(0, channels // GROUP, build, 0)

    taps_s[...] = jnp.zeros_like(taps_s)
    taps_s[0 : st_ref.shape[0], :] = st_ref[...]

    @pl.when(seq == 0)
    def _():
        fhalo[...] = jnp.zeros_like(fhalo)
        phalo[...] = jnp.zeros_like(phalo)

    feat_copy.wait()

    @pl.when(has_prev)
    def _():
        feature_halo.wait_recv()

    def short(part, b):
        start = pl.multiple_of(part * channels + b * LANES, LANES)
        groups = taps_s[:, part * LANES : (part + 1) * LANES]
        index = b * per_block + lane[0:8] // GROUP
        taps = jnp.take_along_axis(groups, index, axis=1)
        own = feat[:, pl.ds(start, LANES)].astype(F32)
        before = fhalo[:, pl.ds(start, LANES)].astype(F32)
        joined = jnp.concatenate([before[halo_rows - 8 :], own], axis=0)
        total = taps[0:1] * own
        for j in range(1, st_ref.shape[0]):
            total = total + taps[j : j + 1] * pltpu.roll(joined, j, 0)[8:]
        return total

    def short_block(b, carry):
        at = pl.ds(pl.multiple_of(b * LANES, LANES), LANES)
        qf[:, at] = short(0, b)
        pown[:, at] = (short(1, b) * short(2, b)).astype(BF16)
        return carry

    def product_copy(k):
        at = pl.ds(chunk * k, chunk)
        return remote(
            pown.at[:, at], phalo.at[:, at], ph_sem.at[0, k], ph_sem.at[1, k], following
        )

    early = {1: [(1, 0)], 3: [(1, 1), (2, 0)]}
    for k in range(CHUNKS):
        lax.fori_loop(k * blocks, (k + 1) * blocks, short_block, 0)

        @pl.when(has_next)
        def _():
            product_copy(k).start()

        for slot, piece_index in early.get(k, []):
            relay(slot, piece_index)

    def long_block(b, carry):
        at = pl.ds(pl.multiple_of(b * LANES, LANES), LANES)
        past = phalo[:, at]
        here = pown[:, at]
        stack = jnp.concatenate([past, here, past, here], axis=0)
        matrix = toep[pl.ds(b * per_block, per_block)].reshape(per_block * rows, 4 * LANES)
        every = jnp.dot(matrix, stack, preferred_element_type=F32)
        mixed = every[0:rows]
        for g in range(1, per_block):
            mixed = jnp.where(
                lane // GROUP == g, every[g * rows : (g + 1) * rows], mixed
            )
        gat[0, :, at] = (qf[:, at] * mixed).astype(BF16)
        return carry

    def gate_copy(kind, k):
        at = pl.ds(chunk * k, chunk)
        source, slot, target = ((0, 1, pool[1]), (0, 2, pool[2]), (2, 3, pool[1]))[kind]
        return remote(
            gat.at[source, :, at],
            gat.at[slot, :, at],
            g_sem.at[0, kind, k],
            g_sem.at[1, kind, k],
            target,
        )

    middle = {0: [(1, 2), (2, 1)], 1: [(1, 3)], 2: [(2, 2)], 3: [(2, 3)]}
    for k in range(CHUNKS):

        @pl.when(has_prev)
        def _():
            product_copy(k).wait_recv()

        lax.fori_loop(k * blocks, (k + 1) * blocks, long_block, 0)
        gate_copy(1, k).start()
        gate_copy(0, k).start()
        for slot, piece_index in middle.get(k, []):
            relay(slot, piece_index)

    for k in range(CHUNKS):
        gate_copy(1, k).wait_recv()
        gate_copy(2, k).start()
    for k in range(CHUNKS):
        gate_copy(0, k).wait_recv()
    for k in range(CHUNKS):
        gate_copy(2, k).wait_recv()

    quarters = (y_hi, hi_outer, (y_hi - delta + 4) % 4, (y_hi + 2) % 4)

    def result_copy(slot, member):
        column = pl.multiple_of((quarters[slot] * 2 + core) * shard + half * p, half)
        return remote(
            res.at[slot, member - 1],
            out_ref.at[0, :, pl.ds(column, half)],
            o_sem.at[0, slot, member - 1],
            o_sem.at[1, slot, member - 1],
            pool[member],
        )

    late = {0: [(3, 0), (3, 1)], 1: [(3, 2)], 2: [(3, 3)]}
    for slot in range(4):
        if slot == 0:
            for copy in own_w:
                copy.wait()
        else:
            for k in range(PIECES):
                x_copy(slot, k).wait_recv()
        weights = jnp.concatenate([wbuf[slot, 0], wbuf[slot, 1]], axis=1)
        total = jnp.dot(
            gat[...].reshape(4 * rows, channels), weights, preferred_element_type=F32
        ).astype(BF16)
        for member in (3, 2, 1):
            res[slot, member - 1] = total[member * rows : (member + 1) * rows]
            result_copy(slot, member).start()
        column = pl.multiple_of((quarters[slot] * 2 + core) * shard + half * p, half)
        out_ref[0, :, pl.ds(column, half)] = total[0:rows]
        for later_slot, piece_index in late.get(slot, []):
            relay(later_slot, piece_index)

    for slot in range(4):
        for member in (3, 2, 1):
            result_copy(slot, member).wait_recv()
    for slot in range(4):
        for member in (3, 2, 1):
            result_copy(slot, member).wait_send()
    for slot in range(1, 4):
        for k in range(PIECES):
            y_copy(slot, k).wait_send()
            x_copy(slot, k).wait_send()
    for kind in range(3):
        for k in range(CHUNKS):
            gate_copy(kind, k).wait_send()

    @pl.when(has_next)
    def _():
        feature_halo.wait_send()
        for k in range(CHUNKS):
            product_copy(k).wait_send()


def on_device(seq_count, features, short_taps, long_taps, out_weight):
    rows = features.shape[1]
    channels = features.shape[2] // 3
    depth, shard = out_weight.shape
    width = shard * 8
    dma = pltpu.SemaphoreType.DMA
    whole = pl.BlockSpec(memory_space=pltpu.VMEM)
    anywhere = pl.BlockSpec(memory_space=pl.ANY)
    return pl.pallas_call(
        functools.partial(kernel, seq_count),
        out_shape=jax.ShapeDtypeStruct((1, rows, width), BF16),
        in_specs=[anywhere, whole, whole, anywhere],
        out_specs=whole,
        scratch_shapes=[
            pltpu.VMEM((rows, 3 * channels), BF16),
            pltpu.VMEM((16, 3 * channels), BF16),
            pltpu.VMEM((8, short_taps.shape[1]), F32),
            pltpu.VMEM((LANES, LANES), F32),
            pltpu.VMEM((channels // GROUP, rows, 4 * LANES), BF16),
            pltpu.VMEM((rows, channels), F32),
            pltpu.VMEM((rows, channels), BF16),
            pltpu.VMEM((rows, channels), BF16),
            pltpu.VMEM((4, 2, depth, LANES), BF16),
            pltpu.VMEM((4, rows, channels), BF16),
            pltpu.VMEM((4, 3, rows, shard // 2), BF16),
            dma((3,)),
            dma((2,)),
            dma((2, CHUNKS)),
            dma((2, 3, PIECES)),
            dma((2, 3, PIECES)),
            dma((2, 3, CHUNKS)),
            dma((2, 4, 3)),
        ],
        compiler_params=pltpu.CompilerParams(
            collective_id=0, has_side_effects=True, vmem_limit_bytes=56 * 1024 * 1024
        ),
    )(features, short_taps, long_taps, out_weight)


def solution(mesh):
    in_specs = (P("fsdp", "seq", None), P(), P(), P(None, "fsdp"))
    out_specs = P("fsdp", "seq", None)
    return jax.shard_map(
        functools.partial(on_device, mesh.shape["seq"]),
        mesh=mesh,
        in_specs=in_specs,
        out_specs=out_specs,
        check_vma=False,
    )
```

```python
import functools

import jax
import jax.numpy as jnp
from jax import lax
from jax.experimental import pallas as pl
from jax.experimental.pallas import tpu as pltpu
from jax.sharding import PartitionSpec as P

MESH = pl.DeviceIdType.MESH
GROUP = 16
XN = 4
ZN = 8
LANES = 128
PIECES = 4
CHUNKS = 4
TILE = 32
TO_RIGHT = 1
BF16 = jnp.bfloat16
F32 = jnp.float32


def kernel(
    seq_count,
    x_hbm,
    st_ref,
    lt_ref,
    w_hbm,
    out_ref,
    feat,
    fhalo,
    taps_s,
    tables,
    toep,
    qf,
    pown,
    phalo,
    wown,
    wbuf,
    gat,
    res_own,
    res,
    loc_sem,
    fh_sem,
    ph_sem,
    y_sem,
    x_sem,
    g_sem,
    own_sem,
    o_sem,
):
    rows = feat.shape[0]
    channels = qf.shape[1]
    depth = w_hbm.shape[0]
    shard = w_hbm.shape[1]
    piece = depth // PIECES
    chunk = channels // CHUNKS
    blocks = chunk // LANES
    per_block = LANES // GROUP
    half = shard // 2

    seq = lax.axis_index("seq")
    fs = lax.axis_index("fsdp")
    x = seq % XN
    z = (seq // XN) % ZN
    y_lo = seq // (XN * ZN)
    y_hi = fs // 2
    core = fs % 2
    u = x % 2
    p = z % 2
    delta = 2 * y_lo - 1
    seq_flip = seq - delta * (XN * ZN)
    hi_outer = (y_hi + delta + 4) % 4
    outer = (seq_flip, hi_outer * 2 + core)
    sibling = (seq_flip, fs)
    right = (seq - x + (x + 1) % XN, fs)
    left = (seq - x + (x + XN - 1) % XN, fs)
    seq_z = seq + XN * (1 - 2 * p)
    other = fs + 1 - 2 * core
    pool = (None, (seq, other), (seq_z, fs), (seq_z, other))
    following = (seq + 1, fs)
    previous = (seq - 1, fs)
    has_next = seq < seq_count - 1
    has_prev = seq > 0

    def remote(src, dst, send, recv, target):
        return pltpu.make_async_remote_copy(
            src_ref=src,
            dst_ref=dst,
            send_sem=send,
            recv_sem=recv,
            device_id=target,
            device_id_type=MESH,
        )

    feat_copy = pltpu.make_async_copy(x_hbm.at[0], feat, loc_sem.at[0])
    feat_copy.start()
    own_w = pltpu.make_async_copy(w_hbm, wown, loc_sem.at[1])
    own_w.start()

    barrier = pltpu.get_barrier_semaphore()
    greeted = (outer, sibling, right, left) + pool[1:]
    greeted += (((seq + 1) % seq_count, fs), ((seq + seq_count - 1) % seq_count, fs))
    for target in greeted:
        pl.semaphore_signal(barrier, inc=1, device_id=target, device_id_type=MESH)
    pl.semaphore_wait(barrier, len(greeted))

    halo_rows = fhalo.shape[0]
    feature_halo = remote(
        x_hbm.at[0, pl.ds(rows - halo_rows, halo_rows)],
        fhalo,
        fh_sem.at[0],
        fh_sem.at[1],
        following,
    )

    @pl.when(has_next)
    def _():
        feature_halo.start()

    def y_copy(slot, k):
        at_rows = pl.ds(piece * k, piece)
        if slot == 1:
            column = pl.multiple_of(half * p + LANES * u, LANES)
            src = w_hbm.at[at_rows, pl.ds(column, LANES)]
        else:
            src = wbuf.at[slot - 2, u, at_rows]
        return remote(
            src,
            wbuf.at[slot - 1, u, at_rows],
            y_sem.at[0, slot - 1, k],
            y_sem.at[1, slot - 1, k],
            sibling if slot == 2 else outer,
        )

    def x_copy(slot, k):
        at_rows = pl.ds(piece * k, piece)
        block = wbuf.at[slot - 1, u, at_rows]
        return remote(
            block,
            block,
            x_sem.at[0, slot - 1, k],
            x_sem.at[1, slot - 1, k],
            right if k >= PIECES - TO_RIGHT else left,
        )

    def relay(slot, k):
        y_copy(slot, k).wait_recv()
        if slot < 3:
            y_copy(slot + 1, k).start()
        x_copy(slot, k).start()

    for k in range(PIECES):
        y_copy(1, k).start()

    lane = lax.broadcasted_iota(jnp.int32, (LANES, LANES), 1)
    taps_back = jnp.take_along_axis(lt_ref[...].T, (LANES - lane) % LANES, axis=1)
    high = taps_back.astype(BF16).astype(F32)
    low = taps_back - high
    tables[0] = high
    tables[1] = low
    tables[2] = jnp.where((lane >= 1) & (lane <= TILE), pltpu.roll(low, TILE, 1), high)
    tile_lane = lax.broadcasted_iota(jnp.int32, (TILE, LANES), 1)
    tile_row = lax.broadcasted_iota(jnp.int32, (TILE, LANES), 0)
    before_tile = tile_lane > tile_row
    in_tile = ((tile_lane < TILE) & (tile_lane <= tile_row)) | (
        (tile_lane >= TILE) & (tile_lane < 2 * TILE) & (tile_lane - TILE <= tile_row)
    )

    def circulant(table, g, keep):
        spread = jnp.broadcast_to(tables[table, pl.ds(g, 1), :], (TILE, LANES))
        turned = pltpu.roll(spread, 0, 1, stride=1, stride_axis=0)
        return jnp.where(keep, turned, jnp.zeros_like(turned)).astype(BF16)

    def build(g, carry):
        toep[g, :, 0:128] = circulant(0, g, before_tile)
        toep[g, :, 128:256] = circulant(1, g, before_tile)
        toep[g, :, 256:384] = circulant(2, g, in_tile)
        return carry

    lax.fori_loop(0, channels // GROUP, build, 0, unroll=16)

    taps_s[...] = jnp.zeros_like(taps_s)
    taps_s[0 : st_ref.shape[0], :] = st_ref[...]

    @pl.when(seq == 0)
    def _():
        fhalo[...] = jnp.zeros_like(fhalo)
        phalo[...] = jnp.zeros_like(phalo)

    feat_copy.wait()

    @pl.when(has_prev)
    def _():
        feature_halo.wait_recv()

    def short(part, b):
        start = pl.multiple_of(part * channels + b * LANES, LANES)
        groups = taps_s[:, part * LANES : (part + 1) * LANES]
        index = b * per_block + lane[0:8] // GROUP
        taps = jnp.take_along_axis(groups, index, axis=1)
        own = feat[:, pl.ds(start, LANES)].astype(F32)
        before = fhalo[:, pl.ds(start, LANES)].astype(F32)
        joined = jnp.concatenate([before[halo_rows - 8 :], own], axis=0)
        total = taps[0:1] * own
        for j in range(1, st_ref.shape[0]):
            total = total + taps[j : j + 1] * pltpu.roll(joined, j, 0)[8:]
        return total

    def short_block(b, carry):
        at = pl.ds(pl.multiple_of(b * LANES, LANES), LANES)
        qf[:, at] = short(0, b)
        pown[:, at] = (short(1, b) * short(2, b)).astype(BF16)
        return carry

    def product_copy(k):
        at = pl.ds(chunk * k, chunk)
        return remote(
            pown.at[:, at], phalo.at[:, at], ph_sem.at[0, k], ph_sem.at[1, k], following
        )

    early = {3: [(1, 0)]}
    for k in range(CHUNKS):
        lax.fori_loop(k * blocks, (k + 1) * blocks, short_block, 0)

        @pl.when(has_next)
        def _():
            product_copy(k).start()

        for slot, piece_index in early.get(k, []):
            relay(slot, piece_index)

    def long_block(b, carry):
        at = pl.ds(pl.multiple_of(b * LANES, LANES), LANES)
        joined = jnp.concatenate([phalo[:, at], pown[:, at]], axis=0)
        matrix = toep[pl.ds(b * per_block, per_block)].reshape(per_block * TILE, 3 * LANES)
        matrix = matrix[:, : 2 * LANES + 2 * TILE]
        for tile in range(0, rows, TILE):
            before = joined[tile : tile + LANES]
            here = joined[tile + LANES : tile + LANES + TILE]
            stack = jnp.concatenate([before, before, here, here], axis=0)
            every = jnp.dot(matrix, stack, preferred_element_type=F32)
            mixed = every[0:TILE]
            for g in range(1, per_block):
                mixed = jnp.where(
                    tile_lane // GROUP == g, every[g * TILE : (g + 1) * TILE], mixed
                )
            at_rows = pl.ds(tile, TILE)
            gat[0, at_rows, at] = (qf[at_rows, at] * mixed).astype(BF16)
        return carry

    def gate_copy(kind, k):
        at = pl.ds(chunk * k, chunk)
        source, slot, target = ((0, 1, pool[1]), (0, 2, pool[2]), (2, 3, pool[1]))[kind]
        return remote(
            gat.at[source, :, at],
            gat.at[slot, :, at],
            g_sem.at[0, kind, k],
            g_sem.at[1, kind, k],
            target,
        )

    middle = {
        0: [(1, 1), (2, 0)],
        1: [(1, 2), (2, 1)],
        2: [(1, 3), (2, 2), (3, 0)],
        3: [(2, 3)],
    }
    for k in range(CHUNKS):

        @pl.when(has_prev)
        def _():
            product_copy(k).wait_recv()

        lax.fori_loop(k * blocks, (k + 1) * blocks, long_block, 0)
        gate_copy(1, k).start()
        gate_copy(0, k).start()
        for slot, piece_index in middle[k]:
            relay(slot, piece_index)
        if k > 0:
            gate_copy(1, k - 1).wait_recv()
            gate_copy(2, k - 1).start()

    quarters = (y_hi, hi_outer, (y_hi - delta + 4) % 4, (y_hi + 2) % 4)
    own_column = pl.multiple_of(fs * shard, shard)
    own_result = remote(
        res_own, out_ref.at[0, :, pl.ds(own_column, shard)], own_sem.at[0], own_sem.at[1], pool[1]
    )

    def result_column(slot):
        return pl.multiple_of((quarters[slot] * 2 + core) * shard + half * p, half)

    def result_copy(slot, member):
        return remote(
            res.at[slot - 1, member - 1],
            out_ref.at[0, :, pl.ds(result_column(slot), half)],
            o_sem.at[0, slot - 1, member - 1],
            o_sem.at[1, slot - 1, member - 1],
            pool[member],
        )

    own_w.wait()
    for k in range(CHUNKS):
        gate_copy(0, k).wait_recv()
    total = jnp.dot(
        gat[0:2].reshape(2 * rows, channels), wown[...], preferred_element_type=F32
    ).astype(BF16)
    res_own[...] = total[rows:]
    own_result.start()
    out_ref[0, :, pl.ds(own_column, shard)] = total[0:rows]

    gate_copy(1, CHUNKS - 1).wait_recv()
    gate_copy(2, CHUNKS - 1).start()
    relay(3, 1)
    for k in range(CHUNKS):
        gate_copy(2, k).wait_recv()

    late = {1: [(3, 2)], 2: [(3, 3)], 3: []}
    for slot in range(1, 4):
        for k in range(PIECES):
            x_copy(slot, k).wait_recv()
        weights = jnp.concatenate([wbuf[slot - 1, 0], wbuf[slot - 1, 1]], axis=1)
        total = jnp.dot(
            gat[...].reshape(4 * rows, channels), weights, preferred_element_type=F32
        ).astype(BF16)
        for member in (3, 2, 1):
            res[slot - 1, member - 1] = total[member * rows : (member + 1) * rows]
            result_copy(slot, member).start()
        out_ref[0, :, pl.ds(result_column(slot), half)] = total[0:rows]
        for later_slot, piece_index in late[slot]:
            relay(later_slot, piece_index)

    own_result.wait()
    for slot in range(1, 4):
        for member in (3, 2, 1):
            result_copy(slot, member).wait_recv()
    for slot in range(1, 4):
        for member in (3, 2, 1):
            result_copy(slot, member).wait_send()
    for slot in range(1, 4):
        for k in range(PIECES):
            y_copy(slot, k).wait_send()
            x_copy(slot, k).wait_send()
    for kind in range(3):
        for k in range(CHUNKS):
            gate_copy(kind, k).wait_send()

    @pl.when(has_next)
    def _():
        feature_halo.wait_send()
        for k in range(CHUNKS):
            product_copy(k).wait_send()


def in_hbm(array):
    return pltpu.with_memory_space_constraint(array, pltpu.HBM)


def on_device(seq_count, features, short_taps, long_taps, out_weight):
    rows = features.shape[1]
    channels = features.shape[2] // 3
    depth, shard = out_weight.shape
    width = shard * 8
    dma = pltpu.SemaphoreType.DMA
    whole = pl.BlockSpec(memory_space=pltpu.VMEM)
    anywhere = pl.BlockSpec(memory_space=pltpu.HBM)
    return pl.pallas_call(
        functools.partial(kernel, seq_count),
        out_shape=jax.ShapeDtypeStruct((1, rows, width), BF16),
        in_specs=[anywhere, whole, whole, anywhere],
        out_specs=whole,
        scratch_shapes=[
            pltpu.VMEM((rows, 3 * channels), BF16),
            pltpu.VMEM((16, 3 * channels), BF16),
            pltpu.VMEM((8, short_taps.shape[1]), F32),
            pltpu.VMEM((3, LANES, LANES), F32),
            pltpu.VMEM((channels // GROUP, TILE, 3 * LANES), BF16),
            pltpu.VMEM((rows, channels), F32),
            pltpu.VMEM((rows, channels), BF16),
            pltpu.VMEM((rows, channels), BF16),
            pltpu.VMEM((depth, shard), BF16),
            pltpu.VMEM((3, 2, depth, LANES), BF16),
            pltpu.VMEM((4, rows, channels), BF16),
            pltpu.VMEM((rows, shard), BF16),
            pltpu.VMEM((3, 3, rows, shard // 2), BF16),
            dma((2,)),
            dma((2,)),
            dma((2, CHUNKS)),
            dma((2, 3, PIECES)),
            dma((2, 3, PIECES)),
            dma((2, 3, CHUNKS)),
            dma((2,)),
            dma((2, 3, 3)),
        ],
        compiler_params=pltpu.CompilerParams(
            collective_id=0, has_side_effects=True, vmem_limit_bytes=28 * 1024 * 1024
        ),
    )(in_hbm(features), short_taps, long_taps, in_hbm(out_weight))


def solution(mesh):
    in_specs = (P("fsdp", "seq", None), P(), P(), P(None, "fsdp"))
    out_specs = P("fsdp", "seq", None)
    return jax.shard_map(
        functools.partial(on_device, mesh.shape["seq"]),
        mesh=mesh,
        in_specs=in_specs,
        out_specs=out_specs,
        check_vma=False,
    )
```

```python
import functools

import jax
import jax.numpy as jnp
from jax import lax
from jax.experimental import pallas as pl
from jax.experimental.pallas import tpu as pltpu
from jax.sharding import PartitionSpec as P

MESH = pl.DeviceIdType.MESH
GROUP = 16
XN = 4
ZN = 8
LANES = 128
PIECES = 4
CHUNKS = 4
TILE = 32
TO_RIGHT = 1
BF16 = jnp.bfloat16
F32 = jnp.float32


def kernel(
    seq_count,
    x_hbm,
    st_ref,
    lt_ref,
    w_hbm,
    out_ref,
    feat,
    fhalo,
    taps_s,
    tables,
    toep,
    qf,
    pown,
    phalo,
    wown,
    wbuf,
    gat,
    res_own,
    res,
    loc_sem,
    fh_sem,
    ph_sem,
    y_sem,
    x_sem,
    g_sem,
    own_sem,
    o_sem,
):
    rows = feat.shape[0]
    channels = qf.shape[1]
    depth = w_hbm.shape[0]
    shard = w_hbm.shape[1]
    piece = depth // PIECES
    chunk = channels // CHUNKS
    blocks = chunk // LANES
    per_block = LANES // GROUP
    half = shard // 2

    seq = lax.axis_index("seq")
    fs = lax.axis_index("fsdp")
    x = seq % XN
    z = (seq // XN) % ZN
    y_lo = seq // (XN * ZN)
    y_hi = fs // 2
    core = fs % 2
    u = x % 2
    p = z % 2
    delta = 2 * y_lo - 1
    seq_flip = seq - delta * (XN * ZN)
    hi_outer = (y_hi + delta + 4) % 4
    outer = (seq_flip, hi_outer * 2 + core)
    sibling = (seq_flip, fs)
    right = (seq - x + (x + 1) % XN, fs)
    left = (seq - x + (x + XN - 1) % XN, fs)
    seq_z = seq + XN * (1 - 2 * p)
    other = fs + 1 - 2 * core
    pool = (None, (seq, other), (seq_z, fs), (seq_z, other))
    following = (seq + 1, fs)
    previous = (seq - 1, fs)
    has_next = seq < seq_count - 1
    has_prev = seq > 0

    def remote(src, dst, send, recv, target):
        return pltpu.make_async_remote_copy(
            src_ref=src,
            dst_ref=dst,
            send_sem=send,
            recv_sem=recv,
            device_id=target,
            device_id_type=MESH,
        )

    feat_copy = pltpu.make_async_copy(x_hbm.at[0], feat, loc_sem.at[0])
    feat_copy.start()
    own_w = pltpu.make_async_copy(w_hbm, wown, loc_sem.at[1])
    own_w.start()

    barrier = pltpu.get_barrier_semaphore()
    greeted = (outer, sibling, right, left) + pool[1:]
    greeted += (((seq + 1) % seq_count, fs), ((seq + seq_count - 1) % seq_count, fs))
    for target in greeted:
        pl.semaphore_signal(barrier, inc=1, device_id=target, device_id_type=MESH)
    pl.semaphore_wait(barrier, len(greeted))

    halo_rows = fhalo.shape[0]
    feature_halo = remote(
        x_hbm.at[0, pl.ds(rows - halo_rows, halo_rows)],
        fhalo,
        fh_sem.at[0],
        fh_sem.at[1],
        following,
    )

    @pl.when(has_next)
    def _():
        feature_halo.start()

    def y_copy(slot, k):
        at_rows = pl.ds(piece * k, piece)
        if slot == 1:
            column = pl.multiple_of(half * p + LANES * u, LANES)
            src = w_hbm.at[at_rows, pl.ds(column, LANES)]
        else:
            src = wbuf.at[slot - 2, u, at_rows]
        return remote(
            src,
            wbuf.at[slot - 1, u, at_rows],
            y_sem.at[0, slot - 1, k],
            y_sem.at[1, slot - 1, k],
            sibling if slot == 2 else outer,
        )

    def x_copy(slot, k):
        at_rows = pl.ds(piece * k, piece)
        block = wbuf.at[slot - 1, u, at_rows]
        return remote(
            block,
            block,
            x_sem.at[0, slot - 1, k],
            x_sem.at[1, slot - 1, k],
            right if k >= PIECES - TO_RIGHT else left,
        )

    def relay(slot, k):
        y_copy(slot, k).wait_recv()
        if slot < 3:
            y_copy(slot + 1, k).start()
        x_copy(slot, k).start()

    for k in range(PIECES):
        y_copy(1, k).start()

    lane = lax.broadcasted_iota(jnp.int32, (LANES, LANES), 1)
    taps_back = jnp.take_along_axis(lt_ref[...].T, (LANES - lane) % LANES, axis=1)
    high = taps_back.astype(BF16).astype(F32)
    low = taps_back - high
    tables[0] = high
    tables[1] = low
    tables[2] = jnp.where((lane >= 1) & (lane <= TILE), pltpu.roll(low, TILE, 1), high)
    tile_lane = lax.broadcasted_iota(jnp.int32, (TILE, LANES), 1)
    tile_row = lax.broadcasted_iota(jnp.int32, (TILE, LANES), 0)
    before_tile = tile_lane > tile_row
    in_tile = ((tile_lane < TILE) & (tile_lane <= tile_row)) | (
        (tile_lane >= TILE) & (tile_lane < 2 * TILE) & (tile_lane - TILE <= tile_row)
    )

    def circulant(table, g, keep):
        spread = jnp.broadcast_to(tables[table, pl.ds(g, 1), :], (TILE, LANES))
        turned = pltpu.roll(spread, 0, 1, stride=1, stride_axis=0)
        return jnp.where(keep, turned, jnp.zeros_like(turned)).astype(BF16)

    def build(g, carry):
        toep[g, :, 0:128] = circulant(0, g, before_tile)
        toep[g, :, 128:256] = circulant(1, g, before_tile)
        toep[g, :, 256:384] = circulant(2, g, in_tile)
        return carry

    lax.fori_loop(0, channels // GROUP, build, 0, unroll=16)

    taps_s[...] = jnp.zeros_like(taps_s)
    taps_s[0 : st_ref.shape[0], :] = st_ref[...]

    @pl.when(seq == 0)
    def _():
        fhalo[...] = jnp.zeros_like(fhalo)
        phalo[...] = jnp.zeros_like(phalo)

    feat_copy.wait()

    @pl.when(has_prev)
    def _():
        feature_halo.wait_recv()

    def short(part, b):
        start = pl.multiple_of(part * channels + b * LANES, LANES)
        groups = taps_s[:, part * LANES : (part + 1) * LANES]
        index = b * per_block + lane[0:8] // GROUP
        taps = jnp.take_along_axis(groups, index, axis=1)
        own = feat[:, pl.ds(start, LANES)].astype(F32)
        before = fhalo[:, pl.ds(start, LANES)].astype(F32)
        joined = jnp.concatenate([before[halo_rows - 8 :], own], axis=0)
        total = taps[0:1] * own
        for j in range(1, st_ref.shape[0]):
            total = total + taps[j : j + 1] * pltpu.roll(joined, j, 0)[8:]
        return total

    def short_block(b, carry):
        at = pl.ds(pl.multiple_of(b * LANES, LANES), LANES)
        qf[:, at] = short(0, b)
        pown[:, at] = (short(1, b) * short(2, b)).astype(BF16)
        return carry

    def product_copy(k):
        at = pl.ds(chunk * k, chunk)
        return remote(
            pown.at[:, at], phalo.at[:, at], ph_sem.at[0, k], ph_sem.at[1, k], following
        )

    early = {3: [(1, 0)]}
    for k in range(CHUNKS):
        lax.fori_loop(k * blocks, (k + 1) * blocks, short_block, 0)

        @pl.when(has_next)
        def _():
            product_copy(k).start()

        for slot, piece_index in early.get(k, []):
            relay(slot, piece_index)

    def long_block(b, carry):
        at = pl.ds(pl.multiple_of(b * LANES, LANES), LANES)
        joined = jnp.concatenate([phalo[:, at], pown[:, at]], axis=0)
        matrix = toep[pl.ds(b * per_block, per_block)].reshape(per_block * TILE, 3 * LANES)
        matrix = matrix[:, : 2 * LANES + 2 * TILE]
        for tile in range(0, rows, TILE):
            before = joined[tile : tile + LANES]
            here = joined[tile + LANES : tile + LANES + TILE]
            stack = jnp.concatenate([before, before, here, here], axis=0)
            every = jnp.dot(matrix, stack, preferred_element_type=F32)
            mixed = every[0:TILE]
            for g in range(1, per_block):
                mixed = jnp.where(
                    tile_lane // GROUP == g, every[g * TILE : (g + 1) * TILE], mixed
                )
            at_rows = pl.ds(tile, TILE)
            gat[0, at_rows, at] = (qf[at_rows, at] * mixed).astype(BF16)
        return carry

    def gate_copy(kind, k):
        at = pl.ds(chunk * k, chunk)
        source, slot, target = ((0, 1, pool[1]), (0, 2, pool[2]), (2, 3, pool[1]))[kind]
        return remote(
            gat.at[source, :, at],
            gat.at[slot, :, at],
            g_sem.at[0, kind, k],
            g_sem.at[1, kind, k],
            target,
        )

    middle = {
        0: [(1, 1), (2, 0)],
        1: [(1, 2), (2, 1)],
        2: [(1, 3), (2, 2), (3, 0)],
        3: [(2, 3)],
    }
    for k in range(CHUNKS):

        @pl.when(has_prev)
        def _():
            product_copy(k).wait_recv()

        lax.fori_loop(k * blocks, (k + 1) * blocks, long_block, 0)
        gate_copy(1, k).start()
        gate_copy(0, k).start()
        for slot, piece_index in middle[k]:
            relay(slot, piece_index)
        if k > 0:
            gate_copy(1, k - 1).wait_recv()
            gate_copy(2, k - 1).start()

    quarters = (y_hi, hi_outer, (y_hi - delta + 4) % 4, (y_hi + 2) % 4)
    own_column = pl.multiple_of(fs * shard, shard)
    own_result = remote(
        res_own, out_ref.at[0, :, pl.ds(own_column, shard)], own_sem.at[0], own_sem.at[1], pool[1]
    )

    def result_column(slot):
        return pl.multiple_of((quarters[slot] * 2 + core) * shard + half * p, half)

    def result_copy(slot, member):
        return remote(
            res.at[slot - 1, member - 1],
            out_ref.at[0, :, pl.ds(result_column(slot), half)],
            o_sem.at[0, slot - 1, member - 1],
            o_sem.at[1, slot - 1, member - 1],
            pool[member],
        )

    own_w.wait()
    for k in range(CHUNKS):
        gate_copy(0, k).wait_recv()
    total = jnp.dot(
        gat[0:2].reshape(2 * rows, channels), wown[...], preferred_element_type=F32
    ).astype(BF16)
    res_own[...] = total[rows:]
    own_result.start()
    out_ref[0, :, pl.ds(own_column, shard)] = total[0:rows]

    gate_copy(1, CHUNKS - 1).wait_recv()
    gate_copy(2, CHUNKS - 1).start()
    relay(3, 1)
    for k in range(CHUNKS):
        gate_copy(2, k).wait_recv()

    late = {1: [(3, 2)], 2: [(3, 3)], 3: []}
    for slot in range(1, 4):
        for k in range(PIECES):
            x_copy(slot, k).wait_recv()
        weights = jnp.concatenate([wbuf[slot - 1, 0], wbuf[slot - 1, 1]], axis=1)
        total = jnp.dot(
            gat[...].reshape(4 * rows, channels), weights, preferred_element_type=F32
        ).astype(BF16)
        for member in (3, 2, 1):
            res[slot - 1, member - 1] = total[member * rows : (member + 1) * rows]
            result_copy(slot, member).start()
        out_ref[0, :, pl.ds(result_column(slot), half)] = total[0:rows]
        for later_slot, piece_index in late[slot]:
            relay(later_slot, piece_index)

    own_result.wait()
    for slot in range(1, 4):
        for member in (3, 2, 1):
            result_copy(slot, member).wait_recv()
    for slot in range(1, 4):
        for member in (3, 2, 1):
            result_copy(slot, member).wait_send()
    for slot in range(1, 4):
        for k in range(PIECES):
            y_copy(slot, k).wait_send()
            x_copy(slot, k).wait_send()
    for kind in range(3):
        for k in range(CHUNKS):
            gate_copy(kind, k).wait_send()

    @pl.when(has_next)
    def _():
        feature_halo.wait_send()
        for k in range(CHUNKS):
            product_copy(k).wait_send()


def in_hbm(array):
    return pltpu.with_memory_space_constraint(array, pltpu.HBM)


def on_device(seq_count, features, short_taps, long_taps, out_weight):
    rows = features.shape[1]
    channels = features.shape[2] // 3
    depth, shard = out_weight.shape
    width = shard * 8
    dma = pltpu.SemaphoreType.DMA
    whole = pl.BlockSpec(memory_space=pltpu.VMEM)
    anywhere = pl.BlockSpec(memory_space=pltpu.HBM)
    return pl.pallas_call(
        functools.partial(kernel, seq_count),
        out_shape=jax.ShapeDtypeStruct((1, rows, width), BF16),
        in_specs=[anywhere, whole, whole, anywhere],
        out_specs=whole,
        scratch_shapes=[
            pltpu.VMEM((rows, 3 * channels), BF16),
            pltpu.VMEM((8, 3 * channels), BF16),
            pltpu.VMEM((8, short_taps.shape[1]), F32),
            pltpu.VMEM((3, LANES, LANES), F32),
            pltpu.VMEM((channels // GROUP, TILE, 3 * LANES), BF16),
            pltpu.VMEM((rows, channels), F32),
            pltpu.VMEM((rows, channels), BF16),
            pltpu.VMEM((rows, channels), BF16),
            pltpu.VMEM((depth, shard), BF16),
            pltpu.VMEM((3, 2, depth, LANES), BF16),
            pltpu.VMEM((4, rows, channels), BF16),
            pltpu.VMEM((rows, shard), BF16),
            pltpu.VMEM((3, 3, rows, shard // 2), BF16),
            dma((2,)),
            dma((2,)),
            dma((2, CHUNKS)),
            dma((2, 3, PIECES)),
            dma((2, 3, PIECES)),
            dma((2, 3, CHUNKS)),
            dma((2,)),
            dma((2, 3, 3)),
        ],
        compiler_params=pltpu.CompilerParams(
            collective_id=0, has_side_effects=True, vmem_limit_bytes=28 * 1024 * 1024
        ),
    )(in_hbm(features), short_taps, long_taps, in_hbm(out_weight))


def solution(mesh):
    in_specs = (P("fsdp", "seq", None), P(), P(), P(None, "fsdp"))
    out_specs = P("fsdp", "seq", None)
    return jax.shard_map(
        functools.partial(on_device, mesh.shape["seq"]),
        mesh=mesh,
        in_specs=in_specs,
        out_specs=out_specs,
        check_vma=False,
    )
```

```python
import functools

import jax
import jax.numpy as jnp
from jax import lax
from jax.experimental import pallas as pl
from jax.experimental.pallas import tpu as pltpu
from jax.sharding import PartitionSpec as P

MESH = pl.DeviceIdType.MESH
GROUP = 16
XN = 4
ZN = 8
LANES = 128
PIECES = 4
CHUNKS = 4
TILE = 16
TO_RIGHT = 1
BF16 = jnp.bfloat16
F32 = jnp.float32


def kernel(
    seq_count,
    x_hbm,
    st_ref,
    lt_ref,
    w_hbm,
    out_ref,
    feat,
    fhalo,
    taps_s,
    tables,
    toep,
    qf,
    pown,
    phalo,
    wown,
    wbuf,
    gat,
    res_own,
    res,
    loc_sem,
    fh_sem,
    ph_sem,
    y_sem,
    x_sem,
    g_sem,
    own_sem,
    o_sem,
):
    rows = feat.shape[0]
    channels = qf.shape[1]
    depth = w_hbm.shape[0]
    shard = w_hbm.shape[1]
    piece = depth // PIECES
    chunk = channels // CHUNKS
    blocks = chunk // LANES
    per_block = LANES // GROUP
    half = shard // 2

    seq = lax.axis_index("seq")
    fs = lax.axis_index("fsdp")
    x = seq % XN
    z = (seq // XN) % ZN
    y_lo = seq // (XN * ZN)
    y_hi = fs // 2
    core = fs % 2
    u = x % 2
    p = z % 2
    delta = 2 * y_lo - 1
    seq_flip = seq - delta * (XN * ZN)
    hi_outer = (y_hi + delta + 4) % 4
    outer = (seq_flip, hi_outer * 2 + core)
    sibling = (seq_flip, fs)
    right = (seq - x + (x + 1) % XN, fs)
    left = (seq - x + (x + XN - 1) % XN, fs)
    seq_z = seq + XN * (1 - 2 * p)
    other = fs + 1 - 2 * core
    pool = (None, (seq, other), (seq_z, fs), (seq_z, other))
    following = (seq + 1, fs)
    previous = (seq - 1, fs)
    has_next = seq < seq_count - 1
    has_prev = seq > 0

    def remote(src, dst, send, recv, target):
        return pltpu.make_async_remote_copy(
            src_ref=src,
            dst_ref=dst,
            send_sem=send,
            recv_sem=recv,
            device_id=target,
            device_id_type=MESH,
        )

    feat_copy = pltpu.make_async_copy(x_hbm.at[0], feat, loc_sem.at[0])
    feat_copy.start()
    own_w = pltpu.make_async_copy(w_hbm, wown, loc_sem.at[1])
    own_w.start()

    barrier = pltpu.get_barrier_semaphore()
    greeted = (outer, sibling, right, left) + pool[1:]
    greeted += (((seq + 1) % seq_count, fs), ((seq + seq_count - 1) % seq_count, fs))
    for target in greeted:
        pl.semaphore_signal(barrier, inc=1, device_id=target, device_id_type=MESH)
    pl.semaphore_wait(barrier, len(greeted))

    halo_rows = fhalo.shape[0]
    feature_halo = remote(
        x_hbm.at[0, pl.ds(rows - halo_rows, halo_rows)],
        fhalo,
        fh_sem.at[0],
        fh_sem.at[1],
        following,
    )

    @pl.when(has_next)
    def _():
        feature_halo.start()

    def y_copy(slot, k):
        at_rows = pl.ds(piece * k, piece)
        if slot == 1:
            column = pl.multiple_of(half * p + LANES * u, LANES)
            src = w_hbm.at[at_rows, pl.ds(column, LANES)]
        else:
            src = wbuf.at[slot - 2, u, at_rows]
        return remote(
            src,
            wbuf.at[slot - 1, u, at_rows],
            y_sem.at[0, slot - 1, k],
            y_sem.at[1, slot - 1, k],
            sibling if slot == 2 else outer,
        )

    def x_copy(slot, k):
        at_rows = pl.ds(piece * k, piece)
        block = wbuf.at[slot - 1, u, at_rows]
        return remote(
            block,
            block,
            x_sem.at[0, slot - 1, k],
            x_sem.at[1, slot - 1, k],
            right if k >= PIECES - TO_RIGHT else left,
        )

    def relay(slot, k):
        y_copy(slot, k).wait_recv()
        if slot < 3:
            y_copy(slot + 1, k).start()
        x_copy(slot, k).start()

    for k in range(PIECES):
        y_copy(1, k).start()

    lane = lax.broadcasted_iota(jnp.int32, (LANES, LANES), 1)
    taps_back = jnp.take_along_axis(lt_ref[...].T, (LANES - lane) % LANES, axis=1)
    high = taps_back.astype(BF16).astype(F32)
    low = taps_back - high
    tables[0] = high
    tables[1] = low
    tables[2] = jnp.where((lane >= 1) & (lane <= TILE), pltpu.roll(low, TILE, 1), high)
    tile_lane = lax.broadcasted_iota(jnp.int32, (TILE, LANES), 1)
    tile_row = lax.broadcasted_iota(jnp.int32, (TILE, LANES), 0)
    before_tile = tile_lane > tile_row
    in_tile = ((tile_lane < TILE) & (tile_lane <= tile_row)) | (
        (tile_lane >= TILE) & (tile_lane < 2 * TILE) & (tile_lane - TILE <= tile_row)
    )

    def circulant(table, g, keep):
        spread = jnp.broadcast_to(tables[table, pl.ds(g, 1), :], (TILE, LANES))
        turned = pltpu.roll(spread, 0, 1, stride=1, stride_axis=0)
        return jnp.where(keep, turned, jnp.zeros_like(turned)).astype(BF16)

    def build(g, carry):
        toep[g, :, 0:128] = circulant(0, g, before_tile)
        toep[g, :, 128:256] = circulant(1, g, before_tile)
        toep[g, :, 256:384] = circulant(2, g, in_tile)
        return carry

    lax.fori_loop(0, channels // GROUP, build, 0, unroll=16)

    taps_s[...] = jnp.zeros_like(taps_s)
    taps_s[0 : st_ref.shape[0], :] = st_ref[...]

    @pl.when(seq == 0)
    def _():
        fhalo[...] = jnp.zeros_like(fhalo)
        phalo[...] = jnp.zeros_like(phalo)

    feat_copy.wait()

    @pl.when(has_prev)
    def _():
        feature_halo.wait_recv()

    def short(part, b):
        start = pl.multiple_of(part * channels + b * LANES, LANES)
        groups = taps_s[:, part * LANES : (part + 1) * LANES]
        index = b * per_block + lane[0:8] // GROUP
        taps = jnp.take_along_axis(groups, index, axis=1)
        own = feat[:, pl.ds(start, LANES)].astype(F32)
        before = fhalo[:, pl.ds(start, LANES)].astype(F32)
        joined = jnp.concatenate([before[halo_rows - 8 :], own], axis=0)
        total = taps[0:1] * own
        for j in range(1, st_ref.shape[0]):
            total = total + taps[j : j + 1] * pltpu.roll(joined, j, 0)[8:]
        return total

    def short_block(b, carry):
        at = pl.ds(pl.multiple_of(b * LANES, LANES), LANES)
        qf[:, at] = short(0, b)
        pown[:, at] = (short(1, b) * short(2, b)).astype(BF16)
        return carry

    def product_copy(k):
        at = pl.ds(chunk * k, chunk)
        return remote(
            pown.at[:, at], phalo.at[:, at], ph_sem.at[0, k], ph_sem.at[1, k], following
        )

    early = {3: [(1, 0)]}
    for k in range(CHUNKS):
        lax.fori_loop(k * blocks, (k + 1) * blocks, short_block, 0)

        @pl.when(has_next)
        def _():
            product_copy(k).start()

        for slot, piece_index in early.get(k, []):
            relay(slot, piece_index)

    def long_block(b, carry):
        at = pl.ds(pl.multiple_of(b * LANES, LANES), LANES)
        joined = jnp.concatenate([phalo[:, at], pown[:, at]], axis=0)
        matrix = toep[pl.ds(b * per_block, per_block)].reshape(per_block * TILE, 3 * LANES)
        matrix = matrix[:, : 2 * LANES + 2 * TILE]
        for tile in range(0, rows, TILE):
            before = joined[tile : tile + LANES]
            here = joined[tile + LANES : tile + LANES + TILE]
            stack = jnp.concatenate([before, before, here, here], axis=0)
            every = jnp.dot(matrix, stack, preferred_element_type=F32)
            mixed = every[0:TILE]
            for g in range(1, per_block):
                mixed = jnp.where(
                    tile_lane // GROUP == g, every[g * TILE : (g + 1) * TILE], mixed
                )
            at_rows = pl.ds(tile, TILE)
            gat[0, at_rows, at] = (qf[at_rows, at] * mixed).astype(BF16)
        return carry

    def gate_copy(kind, k):
        at = pl.ds(chunk * k, chunk)
        source, slot, target = ((0, 1, pool[1]), (0, 2, pool[2]), (2, 3, pool[1]))[kind]
        return remote(
            gat.at[source, :, at],
            gat.at[slot, :, at],
            g_sem.at[0, kind, k],
            g_sem.at[1, kind, k],
            target,
        )

    middle = {
        0: [(1, 1), (2, 0)],
        1: [(1, 2), (2, 1)],
        2: [(1, 3), (2, 2), (3, 0)],
        3: [(2, 3)],
    }
    for k in range(CHUNKS):

        @pl.when(has_prev)
        def _():
            product_copy(k).wait_recv()

        lax.fori_loop(k * blocks, (k + 1) * blocks, long_block, 0)
        gate_copy(1, k).start()
        gate_copy(0, k).start()
        for slot, piece_index in middle[k]:
            relay(slot, piece_index)
        if k > 0:
            gate_copy(1, k - 1).wait_recv()
            gate_copy(2, k - 1).start()

    quarters = (y_hi, hi_outer, (y_hi - delta + 4) % 4, (y_hi + 2) % 4)
    own_column = pl.multiple_of(fs * shard, shard)
    own_result = remote(
        res_own, out_ref.at[0, :, pl.ds(own_column, shard)], own_sem.at[0], own_sem.at[1], pool[1]
    )

    def result_column(slot):
        return pl.multiple_of((quarters[slot] * 2 + core) * shard + half * p, half)

    def result_copy(slot, member):
        return remote(
            res.at[slot - 1, member - 1],
            out_ref.at[0, :, pl.ds(result_column(slot), half)],
            o_sem.at[0, slot - 1, member - 1],
            o_sem.at[1, slot - 1, member - 1],
            pool[member],
        )

    own_w.wait()
    for k in range(CHUNKS):
        gate_copy(0, k).wait_recv()
    total = jnp.dot(
        gat[0:2].reshape(2 * rows, channels), wown[...], preferred_element_type=F32
    ).astype(BF16)
    res_own[...] = total[rows:]
    own_result.start()
    out_ref[0, :, pl.ds(own_column, shard)] = total[0:rows]

    gate_copy(1, CHUNKS - 1).wait_recv()
    gate_copy(2, CHUNKS - 1).start()
    relay(3, 1)
    for k in range(CHUNKS):
        gate_copy(2, k).wait_recv()

    late = {1: [(3, 2)], 2: [(3, 3)], 3: []}
    for slot in range(1, 4):
        for k in range(PIECES):
            x_copy(slot, k).wait_recv()
        weights = jnp.concatenate([wbuf[slot - 1, 0], wbuf[slot - 1, 1]], axis=1)
        total = jnp.dot(
            gat[...].reshape(4 * rows, channels), weights, preferred_element_type=F32
        ).astype(BF16)
        for member in (3, 2, 1):
            res[slot - 1, member - 1] = total[member * rows : (member + 1) * rows]
            result_copy(slot, member).start()
        out_ref[0, :, pl.ds(result_column(slot), half)] = total[0:rows]
        for later_slot, piece_index in late[slot]:
            relay(later_slot, piece_index)

    own_result.wait()
    for slot in range(1, 4):
        for member in (3, 2, 1):
            result_copy(slot, member).wait_recv()
    for slot in range(1, 4):
        for member in (3, 2, 1):
            result_copy(slot, member).wait_send()
    for slot in range(1, 4):
        for k in range(PIECES):
            y_copy(slot, k).wait_send()
            x_copy(slot, k).wait_send()
    for kind in range(3):
        for k in range(CHUNKS):
            gate_copy(kind, k).wait_send()

    @pl.when(has_next)
    def _():
        feature_halo.wait_send()
        for k in range(CHUNKS):
            product_copy(k).wait_send()


def in_hbm(array):
    return pltpu.with_memory_space_constraint(array, pltpu.HBM)


def on_device(seq_count, features, short_taps, long_taps, out_weight):
    rows = features.shape[1]
    channels = features.shape[2] // 3
    depth, shard = out_weight.shape
    width = shard * 8
    dma = pltpu.SemaphoreType.DMA
    whole = pl.BlockSpec(memory_space=pltpu.VMEM)
    anywhere = pl.BlockSpec(memory_space=pltpu.HBM)
    return pl.pallas_call(
        functools.partial(kernel, seq_count),
        out_shape=jax.ShapeDtypeStruct((1, rows, width), BF16),
        in_specs=[anywhere, whole, whole, anywhere],
        out_specs=whole,
        scratch_shapes=[
            pltpu.VMEM((rows, 3 * channels), BF16),
            pltpu.VMEM((8, 3 * channels), BF16),
            pltpu.VMEM((8, short_taps.shape[1]), F32),
            pltpu.VMEM((3, LANES, LANES), F32),
            pltpu.VMEM((channels // GROUP, TILE, 3 * LANES), BF16),
            pltpu.VMEM((rows, channels), F32),
            pltpu.VMEM((rows, channels), BF16),
            pltpu.VMEM((rows, channels), BF16),
            pltpu.VMEM((depth, shard), BF16),
            pltpu.VMEM((3, 2, depth, LANES), BF16),
            pltpu.VMEM((4, rows, channels), BF16),
            pltpu.VMEM((rows, shard), BF16),
            pltpu.VMEM((3, 3, rows, shard // 2), BF16),
            dma((2,)),
            dma((2,)),
            dma((2, CHUNKS)),
            dma((2, 3, PIECES)),
            dma((2, 3, PIECES)),
            dma((2, 3, CHUNKS)),
            dma((2,)),
            dma((2, 3, 3)),
        ],
        compiler_params=pltpu.CompilerParams(
            collective_id=0, has_side_effects=True, vmem_limit_bytes=28 * 1024 * 1024
        ),
    )(in_hbm(features), short_taps, long_taps, in_hbm(out_weight))


def solution(mesh):
    in_specs = (P("fsdp", "seq", None), P(), P(), P(None, "fsdp"))
    out_specs = P("fsdp", "seq", None)
    return jax.shard_map(
        functools.partial(on_device, mesh.shape["seq"]),
        mesh=mesh,
        in_specs=in_specs,
        out_specs=out_specs,
        check_vma=False,
    )
```
